32 devices in a mesh: groups: 2 (over x), row: 16 (over z, y, core).
Axes of the slice: x: 2, y: 2, z: 4, core: 2. Of those that a mesh axis runs over, the one named last changes fastest.
Arguments:
- fine: bfloat16 [2048, 128, 128], P(('groups', 'row')), parts along dimension 0, may hold values from -6 to 6
- parent: bfloat16 [32, 256, 512], P(('groups', 'row')), parts along dimension 0, may hold values from -6 to 6
- coverage: int32 [64, 4], P('groups'), parts along dimension 0, may hold values from 0 to 15
- owner_slot: int32 [32], P('groups'), parts along dimension 0, may hold values from 0 to 15, each once
- w_query: bfloat16 [128, 128], replicated, may hold values from -0.5 to 0.5
- w_key: bfloat16 [512, 128], replicated, may hold values from -0.25 to 0.25
- w_value: bfloat16 [512, 128], replicated, may hold values from -0.25 to 0.25
- norm_gain: float32 [128], replicated, may hold values from 0.1 to 1.9
- conv_weight: bfloat16 [4, 3, 3, 128, 128], replicated, may hold values from -0.25 to 0.25
- conv_bias: float32 [4, 128], replicated, may hold values from -3 to 3
Outputs:
- refined: bfloat16 [2048, 128, 128], P(('groups', 'row')), parts along dimension 0
The draws below stay inside these ranges and needn't reach their ends.
There are 2 independent parts, one for each index of `groups`. The reference program is written for one: setup_inputs(seed, part) draws one part's arguments, and reference() takes and returns one part's arrays. A program takes and returns all parts, laid end to end along the dimension named above; an argument that names none is the same for every part. Nothing has to cross between parts.
Inputs may be any that keep to these rules, and one draw needn't show every extreme that they name: `owner_slot`: each slot exactly once.
All inputs are finite; a program needn't handle non-finite values.
Results may differ from the reference program's by a relative error of at most 0.014.
Values may be sent and summed in bfloat16 or wider, within the bound.
No kernel may reach another device: no remote copies, remote signals or barrier semaphores. Data moves between devices by JAX's collectives and lax.ppermute only.
A program may use at most 128 MiB of HBM per device.

```python
import jax
import jax.numpy as jnp
from jax import lax

C = 128
PD = 512
KR = 256
TILE = 64
TCOLS = 2
COVER = 4
LAYERS = 4
NENC = 16
TILES = 32
GRID_H = 1024
GRID_W = 128
N_ROW = 16


def with_ends(values, rng, least, top_value):
    dims = values.shape
    place = [jax.random.randint(jax.random.fold_in(rng, axis), (), 0, dims[axis]) for axis in range(len(dims))]
    values = values.at[tuple(place)].set(least)
    longest = dims.index(max(dims))
    place[longest] = (place[longest] + 1) % dims[longest]
    return values.at[tuple(place)].set(top_value)


def shard_levels(stream_key, shape, pieces, low, top_value):
    loudness = 1.0
    for dim, blocks in pieces:
        steps = jax.random.uniform(jax.random.fold_in(jax.random.fold_in(stream_key, 6), dim), (blocks,), jnp.float32, low / len(pieces), top_value / len(pieces))
        loudness = loudness * jnp.repeat(jnp.exp(steps), shape[dim] // blocks).reshape((-1,) + (1,) * (len(shape) - 1 - dim))
    return loudness


def noise(stream_key, dims, spread, limit, cuts=(), kind=jnp.bfloat16):
    loudness = shard_levels(stream_key, dims, cuts, -0.22, 0.18) if cuts else 1.0
    array = jax.random.normal(stream_key, dims, jnp.float32) * spread * loudness
    return jnp.minimum(jnp.maximum(array, -limit), limit).astype(kind)


def setup_inputs(seed: int = 0, part: int = 0) -> dict:
    key_of = jax.random.split(jax.random.key(seed), 11)
    part_splits = jax.random.split(jax.random.fold_in(key_of[10], part), 11)
    return {
        "fine": noise(part_splits[0], (GRID_H, GRID_W, C), 1.0, 6.0, ((0, 16),)),
        "parent": noise(part_splits[1], (NENC, KR, PD), 1.0, 6.0, ((0, 16),)),
        "coverage": with_ends(jax.random.randint(part_splits[2], (TILES, COVER), 0, NENC), jax.random.fold_in(part_splits[2], 1), 0, NENC - 1).astype(jnp.int32),
        "owner_slot": jax.random.permutation(part_splits[3], NENC).astype(jnp.int32),
        "w_query": noise(key_of[4], (C, C), C ** -0.5, 0.5),
        "w_key": noise(key_of[5], (PD, C), PD ** -0.5, 0.25),
        "w_value": noise(key_of[6], (PD, C), PD ** -0.5, 0.25),
        "norm_gain": jnp.clip(1.0 + 0.18 * jax.random.normal(key_of[7], (C,), jnp.float32), 0.1, 1.9),
        "conv_weight": noise(key_of[8], (LAYERS, 3, 3, C, C), (9 * C // 2) ** -0.5, 0.25),
        "conv_bias": noise(key_of[9], (LAYERS, C), 0.5, 3.0, (), jnp.float32),
    }


def reference(fine, parent, coverage, owner_slot, w_query, w_key, w_value, norm_gain, conv_weight, conv_bias):
    enc_keys = jnp.dot(parent, w_key, preferred_element_type=jnp.float32).astype(jnp.bfloat16)
    enc_values = jnp.dot(parent, w_value, preferred_element_type=jnp.float32).astype(jnp.bfloat16)
    queries = jnp.dot(fine, w_query, preferred_element_type=jnp.float32).astype(jnp.bfloat16)
    tiled = queries.reshape(N_ROW, TILE, TCOLS, TILE, C).transpose(0, 2, 1, 3, 4).reshape(TILES, TILE * TILE, C)

    def one_tile(packed):
        tile_q, tile_cov = packed
        slots = owner_slot[tile_cov]
        tile_k = enc_keys[slots].reshape(COVER * KR, C).astype(jnp.float32)
        tile_v = enc_values[slots].reshape(COVER * KR, C)
        scores = jnp.dot(tile_q.astype(jnp.float32), tile_k.T, precision=lax.Precision.HIGHEST) / jnp.sqrt(jnp.float32(C))
        probs = jax.nn.softmax(scores, axis=-1).astype(jnp.bfloat16)
        return jnp.dot(probs, tile_v, preferred_element_type=jnp.float32)
    attended = lax.map(one_tile, (tiled, coverage))
    attended = attended.reshape(N_ROW, TCOLS, TILE, TILE, C).transpose(0, 2, 1, 3, 4).reshape(GRID_H, GRID_W, C)
    meansq = lax.optimization_barrier(jnp.mean(attended * attended, axis=-1, keepdims=True))
    mixed = (fine.astype(jnp.float32) + norm_gain * attended * lax.rsqrt(meansq + 1e-06)).astype(jnp.bfloat16)
    current = mixed
    for layer_idx in range(LAYERS):
        conv_out = lax.conv_general_dilated(current[None], conv_weight[layer_idx], (1, 1), 'SAME', dimension_numbers=('NHWC', 'HWIO', 'NHWC'), preferred_element_type=jnp.float32)[0]
        current = jax.nn.silu(conv_out + conv_bias[layer_idx]).astype(jnp.bfloat16)
    return current
```

```python
import functools
import math

import jax
import jax.numpy as jnp
from jax import lax
from jax.experimental import pallas as pl
from jax.experimental.pallas import tpu as pltpu
from jax.sharding import PartitionSpec as P


BF16, F32 = jnp.bfloat16, jnp.float32
VMEM = pl.BlockSpec(memory_space=pltpu.VMEM)
SMEM = pl.BlockSpec(memory_space=pltpu.SMEM)
ANY = pl.BlockSpec(memory_space=pl.ANY)


def encode_kernel(parent_ref, wk_ref, wv_ref, out_ref):
    rows, chans = parent_ref.shape[0], wk_ref.shape[1]
    parent = parent_ref[...]
    keys = jnp.dot(parent, wk_ref[...], preferred_element_type=F32)
    values = jnp.dot(parent, wv_ref[...], preferred_element_type=F32).astype(BF16)
    out_ref[:chans, :] = keys.T.astype(BF16)
    for half in range(rows // chans):
        out_ref[chans:, half * chans : (half + 1) * chans] = values[half * chans : (half + 1) * chans]


def encode(parent, w_key, w_value):
    rows, chans = parent.shape[0], w_key.shape[1]
    return pl.pallas_call(
        encode_kernel,
        out_shape=jax.ShapeDtypeStruct((2 * chans, rows), BF16),
        in_specs=[VMEM] * 3,
        out_specs=VMEM,
        compiler_params=pltpu.CompilerParams(vmem_limit_bytes=8 * 2**20),
        name="encode",
    )(parent, w_key, w_value)


def ring_tables(count):
    per_chip = 2 if count % 2 == 0 else 1
    chips = count // per_chip
    order = list(range(0, chips, 2)) + list(range(1, chips, 2))[::-1]
    place = [0] * chips
    for at, chip in enumerate(order):
        place[chip] = at
    return per_chip, chips, order, place


def gather_blocks(block, count):
    per_chip, chips, order, _ = ring_tables(count)

    def step(array, shift):
        pairs = [
            (order[at] * per_chip + core, order[(at + shift) % chips] * per_chip + core)
            for at in range(chips)
            for core in range(per_chip)
        ]
        return lax.ppermute(array, "row", pairs)

    partner = [(i, i ^ 1) for i in range(count)]
    held = {0: block}
    ahead = behind = block
    up, down = chips // 2, (chips - 1) // 2
    for hop in range(1, up + 1):
        ahead = step(ahead, 1)
        held[chips - hop] = ahead
        if hop <= down:
            behind = step(behind, -1)
            held[hop] = behind
    groups = []
    for offset in range(chips):
        groups.append((held[offset], [offset], 0))
    if per_chip == 2:
        late = chips - up if chips > 1 else 0
        early = [offset for offset in range(chips) if offset != late]
        if early:
            stacked = jnp.stack([held[offset] for offset in early])
            groups.append((lax.ppermute(stacked, "row", partner), early, 1))
        groups.append((lax.ppermute(held[late], "row", partner), [late], 1))
    return groups


def attend_kernel(ranges, step, layout, pick_ref, fine_ref, wq_ref, gain_ref, *rest):
    blocks = rest[: len(layout)]
    outs = rest[len(layout) : len(layout) + len(ranges)]
    keys, values, sem = rest[len(layout) + len(ranges) :]
    tiles, chans, total = keys.shape
    side = fine_ref.shape[1] // tiles
    rows = blocks[0].shape[-1]
    cover = total // rows

    def copies(ref, tile, j):
        at = tile * cover + j
        out = [pltpu.make_async_copy(ref.at[0:chans], keys.at[tile, :, pl.ds(j * rows, rows)], sem.at[at, 0])]
        for half in range(rows // chans):
            out.append(
                pltpu.make_async_copy(
                    ref.at[pl.ds(chans, chans), pl.ds(half * chans, chans)],
                    values.at[tile, pl.ds(j * rows + half * chans, chans), pl.ds(0, chans)],
                    sem.at[at, 1 + half],
                )
            )
        return out

    for tile in range(tiles):
        for j in range(cover):
            for ref, ids in zip(blocks, layout):
                for place, ident in enumerate(ids):

                    @pl.when(pick_ref[tile * cover + j] == ident)
                    def _():
                        for copy in copies(ref.at[place] if len(ref.shape) == 3 else ref, tile, j):
                            copy.start()

    values[:, :, chans:] = jnp.ones((tiles, total, values.shape[2] - chans), BF16)
    first = blocks[0].at[0] if len(blocks[0].shape) == 3 else blocks[0]
    for tile in range(tiles):
        for j in range(cover):
            for copy in copies(first, tile, j):
                copy.wait()
    scale = math.log2(math.e) / math.sqrt(chans)
    gain = gain_ref[...]

    def some(tile, src, out, dst):
        cells = fine_ref[pl.ds(src, step), tile * side : (tile + 1) * side, :].reshape(step * side, chans)
        queries = (jnp.dot(cells, wq_ref[...], preferred_element_type=F32) * scale).astype(BF16)
        scores = jnp.dot(queries, keys[tile], preferred_element_type=F32)
        top = jnp.max(scores, -1, keepdims=True)
        probs = jnp.exp2(scores - top).astype(BF16)
        summed = jnp.dot(probs, values[tile], preferred_element_type=F32)
        attended, weight = summed[:, :chans], summed[:, chans:]
        meansq = jnp.mean(attended * attended, -1, keepdims=True)
        mixed = cells.astype(F32) + gain * attended * lax.rsqrt(meansq + 1e-6 * weight * weight)
        out[pl.ds(dst, step), tile * side : (tile + 1) * side, :] = mixed.astype(BF16).reshape(step, side, chans)

    for (low, high), out in zip(ranges, outs):
        if high - low == step:
            for tile in range(tiles):
                some(tile, low, out, 0)
        else:

            @pl.loop(0, (high - low) // step)
            def _(i):
                for tile in range(tiles):
                    some(tile, low + i * step, out, i * step)


def attend(pick, fine, w_query, gain, groups, ranges, step, cover):
    chans = fine.shape[2]
    tiles = pick.shape[0] // cover
    rows = groups[0][0].shape[-1]
    chips = max(max(offsets) for _, offsets, _ in groups) + 1
    layout = [[other * chips + offset for offset in offsets] for _, offsets, other in groups]
    return pl.pallas_call(
        functools.partial(attend_kernel, ranges, step, layout),
        out_shape=[jax.ShapeDtypeStruct((high - low,) + fine.shape[1:], BF16) for low, high in ranges],
        in_specs=[SMEM] + [VMEM] * 3 + [ANY] * len(groups),
        out_specs=[VMEM] * len(ranges),
        scratch_shapes=[
            pltpu.VMEM((tiles, chans, cover * rows), BF16),
            pltpu.VMEM((tiles, cover * rows, 2 * chans), BF16),
            pltpu.SemaphoreType.DMA((tiles * cover, 1 + rows // chans)),
        ],
        compiler_params=pltpu.CompilerParams(vmem_limit_bytes=40 * 2**20),
        name="attend",
    )(pick, fine, w_query, gain, *[array for array, _, _ in groups])


def paired_weights(kernels):
    zero = jnp.zeros_like(kernels[:, 0])
    wide = lambda a, b: jnp.concatenate([a, b], -1)
    upper = jnp.concatenate([wide(kernels[:, 0], zero), wide(kernels[:, 1], kernels[:, 0])], -2)
    lower = jnp.concatenate([wide(kernels[:, 2], kernels[:, 1]), wide(zero, kernels[:, 2])], -2)
    both = jnp.concatenate([upper, lower], 1)
    return both.reshape(both.shape[0], -1, both.shape[-1])


def silu(x):
    half = 0.5 * x
    return half + half * jnp.tanh(half)


def conv_kernel(group, place_ref, *refs):
    parts, (weight_ref, bias_ref, out_ref, state_a, state_b) = refs[:-5], refs[-5:]
    layers = weight_ref.shape[0]
    cols, chans = out_ref.shape[1:]
    column = lax.broadcasted_iota(jnp.int32, (cols, 1), 0)
    first = place_ref[0] == 0
    last = place_ref[0] == place_ref[1] - 1

    def put(dst, pair, value):
        west = jnp.where(column == 0, 0.0, pltpu.roll(value, 1, 0))
        east = jnp.where(column == cols - 1, 0.0, pltpu.roll(value, cols - 1, 0))
        dst[0, pair] = west.astype(BF16)
        dst[1, pair] = value.astype(BF16)
        dst[2, pair] = east.astype(BF16)

    def take(ref, src, pair):
        put(state_a, pair, jnp.concatenate([ref[2 * src], ref[2 * src + 1]], -1).astype(F32))

    done = 0
    for part in parts:
        count = part.shape[0] // 2
        if count > 4:
            base = done

            @pl.loop(0, count)
            def _(i):
                take(part, i, base + i)
        else:
            for i in range(count):
                take(part, i, done + i)
        done += count

    source, target = state_a, state_b
    pairs = done
    for layer in range(layers):
        pairs -= 1
        bias = bias_ref[layer : layer + 1, :]
        final = layer == layers - 1

        @pl.loop(0, pl.cdiv(pairs, group))
        def _(i):
            at = jnp.minimum(i * group, pairs - group)
            taps = [
                source[shift, pl.ds(at + lower, group)].reshape(group * cols, 2 * chans)
                for lower in range(2)
                for shift in range(3)
            ]
            total = jnp.dot(jnp.concatenate(taps, -1), weight_ref[layer], preferred_element_type=F32)
            value = silu(total + bias)
            for k in range(group):
                one = value[k * cols : (k + 1) * cols]
                if final:
                    rounded = one.astype(BF16)
                    out_ref[2 * (at + k)] = rounded[:, :chans]
                    out_ref[2 * (at + k) + 1] = rounded[:, chans:]
                else:
                    put(target, at + k, one)

        margin = layers - 1 - layer
        if margin:
            blank = jnp.zeros((3, cols, chans), BF16)

            @pl.when(first)
            def _():
                for row in range(margin):
                    target[:, row // 2, :, (row % 2) * chans : (row % 2 + 1) * chans] = blank

            @pl.when(last)
            def _():
                for row in range(2 * pairs - margin, 2 * pairs):
                    target[:, row // 2, :, (row % 2) * chans : (row % 2 + 1) * chans] = blank

        source, target = target, source


def convolve(place, parts, weights, bias, rows):
    cols, chans = parts[0].shape[1:]
    pairs = sum(part.shape[0] for part in parts) // 2
    return pl.pallas_call(
        functools.partial(conv_kernel, 8),
        out_shape=jax.ShapeDtypeStruct((rows, cols, chans), BF16),
        in_specs=[SMEM] + [VMEM] * (len(parts) + 2),
        out_specs=VMEM,
        scratch_shapes=[pltpu.VMEM((3, pairs, cols, 2 * chans), BF16)] * 2,
        compiler_params=pltpu.CompilerParams(vmem_limit_bytes=56 * 2**20),
        name="convolve",
    )(place, *parts, weights, bias)


def on_device(
    fine, parent, coverage, owner_slot, w_query, w_key, w_value, norm_gain, conv_weight, conv_bias
):
    rows = fine.shape[0]
    tiles = fine.shape[1] // rows
    halo = conv_weight.shape[0]
    cover = coverage.shape[1]
    count = lax.axis_size("row")
    position = lax.axis_index("row")

    block = encode(parent[0], w_key, w_value)
    groups = gather_blocks(block, count)

    per_chip, chips, _, place = ring_tables(count)
    table = jnp.asarray(place, jnp.int32)
    slots = jnp.take(owner_slot, lax.dynamic_slice_in_dim(coverage, position * tiles, tiles, 0).reshape(-1))
    offset = jnp.mod(jnp.take(table, slots // per_chip) - jnp.take(table, position // per_chip), chips)
    other = (slots % per_chip != position % per_chip).astype(jnp.int32)
    pick = other * chips + offset

    weights = paired_weights(conv_weight)
    bias = jnp.concatenate([conv_bias, conv_bias], -1)
    gain = norm_gain[None]

    head, tail = attend(pick, fine, w_query, gain, groups, ((0, halo), (rows - halo, rows)), halo, cover)
    north = lax.ppermute(tail, "row", [(i, i + 1) for i in range(count - 1)])
    south = lax.ppermute(head, "row", [(i + 1, i) for i in range(count - 1)])
    (middle,) = attend(pick, fine, w_query, gain, groups, ((halo, rows - halo),), 8, cover)
    where = jnp.stack([position, jnp.int32(count)])
    return convolve(where, [north, head, middle, tail, south], weights, bias, rows)


def solution(mesh):
    placed = (
        P(("groups", "row"), None, None),
        P(("groups", "row"), None, None),
        P("groups", None),
        P("groups"),
        P(),
        P(),
        P(),
        P(),
        P(),
        P(),
    )
    return jax.shard_map(
        on_device,
        mesh=mesh,
        in_specs=placed,
        out_specs=P(("groups", "row"), None, None),
        check_vma=False,
    )
```

```python
import functools
import math

import jax
import jax.numpy as jnp
from jax import lax
from jax.experimental import pallas as pl
from jax.experimental.pallas import tpu as pltpu
from jax.sharding import PartitionSpec as P


BF16, F32 = jnp.bfloat16, jnp.float32
VMEM = pl.BlockSpec(memory_space=pltpu.VMEM)
SMEM = pl.BlockSpec(memory_space=pltpu.SMEM)
ANY = pl.BlockSpec(memory_space=pl.ANY)
HBM = pl.BlockSpec(memory_space=pltpu.HBM)


def encode_kernel(parent_hbm, wk_hbm, wv_hbm, out_ref, parent_ref, wk_ref, wv_ref, sem):
    moves = [
        pltpu.make_async_copy(src, dst, sem.at[i])
        for i, (src, dst) in enumerate(((parent_hbm, parent_ref), (wk_hbm, wk_ref), (wv_hbm, wv_ref)))
    ]
    for move in moves:
        move.start()
    for move in moves:
        move.wait()
    rows, chans = parent_ref.shape[0], wk_ref.shape[1]
    parent = parent_ref[...]
    keys = jnp.dot(parent, wk_ref[...], preferred_element_type=F32)
    values = jnp.dot(parent, wv_ref[...], preferred_element_type=F32).astype(BF16)
    out_ref[:chans, :] = keys.T.astype(BF16)
    for half in range(rows // chans):
        out_ref[chans:, half * chans : (half + 1) * chans] = values[half * chans : (half + 1) * chans]


def encode(parent, w_key, w_value):
    rows, chans = parent.shape[0], w_key.shape[1]
    return pl.pallas_call(
        encode_kernel,
        out_shape=jax.ShapeDtypeStruct((2 * chans, rows), BF16),
        in_specs=[HBM] * 3,
        out_specs=VMEM,
        scratch_shapes=[pltpu.VMEM(a.shape, a.dtype) for a in (parent, w_key, w_value)]
        + [pltpu.SemaphoreType.DMA((3,))],
        compiler_params=pltpu.CompilerParams(vmem_limit_bytes=8 * 2**20),
        name="encode",
    )(parent, w_key, w_value)


def ring_shape(count):
    per_chip = 2 if count % 2 == 0 else 1
    return per_chip, count // per_chip


def ring_place(chip, chips):
    half = lax.div(chip, 2)
    return jnp.where(lax.rem(chip, 2) == 0, half, chips - 1 - half)


def gather_blocks(block, count):
    per_chip, chips = ring_shape(count)
    order = list(range(0, chips, 2)) + list(range(1, chips, 2))[::-1]

    def step(array, shift):
        pairs = [
            (order[at] * per_chip + core, order[(at + shift) % chips] * per_chip + core)
            for at in range(chips)
            for core in range(per_chip)
        ]
        return lax.ppermute(array, "row", pairs)

    held = {0: block}
    ahead = behind = block
    up, down = chips // 2, (chips - 1) // 2
    for hop in range(1, up + 1):
        ahead = step(ahead, 1)
        held[chips - hop] = ahead
        if hop <= down:
            behind = step(behind, -1)
            held[hop] = behind
    own = [held[offset] for offset in range(chips)]
    if per_chip == 1:
        return own
    partner = [(i, i ^ 1) for i in range(count)]
    return own + [lax.ppermute(array, "row", partner) for array in own]


def attend_kernel(ranges, step, count, coverage_ref, owner_ref, fine_ref, wq_ref, gain_ref, *rest):
    blocks = rest[:count]
    outs = rest[count : count + len(ranges)]
    keys, values, sem = rest[count + len(ranges) :]
    tiles, chans, total = keys.shape
    side = fine_ref.shape[1] // tiles
    rows = blocks[0].shape[1]
    cover = total // rows
    per_chip, chips = ring_shape(count)
    position = lax.axis_index("row")
    home = ring_place(lax.div(position, per_chip), chips)
    core = lax.rem(position, per_chip)

    def copies(ref, tile, j):
        at = tile * cover + j
        out = [pltpu.make_async_copy(ref.at[0:chans], keys.at[tile, :, pl.ds(j * rows, rows)], sem.at[at, 0])]
        for half in range(rows // chans):
            out.append(
                pltpu.make_async_copy(
                    ref.at[pl.ds(chans, chans), pl.ds(half * chans, chans)],
                    values.at[tile, pl.ds(j * rows + half * chans, chans), pl.ds(0, chans)],
                    sem.at[at, 1 + half],
                )
            )
        return out

    for tile in range(tiles):
        for j in range(cover):
            slot = owner_ref[coverage_ref[position * tiles + tile, j]]
            offset = ring_place(lax.div(slot, per_chip), chips) - home
            offset = jnp.where(offset < 0, offset + chips, offset)
            same = lax.rem(slot, per_chip) == core
            for side_of in range(per_chip):

                @pl.when(same if side_of == 0 else jnp.logical_not(same))
                def _():
                    for at in range(chips):

                        @pl.when(offset == at)
                        def _():
                            for copy in copies(blocks[side_of * chips + at], tile, j):
                                copy.start()

    values[:, :, chans:] = jnp.ones((tiles, total, values.shape[2] - chans), BF16)
    for tile in range(tiles):
        for j in range(cover):
            for copy in copies(blocks[0], tile, j):
                copy.wait()
    scale = math.log2(math.e) / math.sqrt(chans)
    gain = gain_ref[...]

    def some(tile, src, out, dst):
        cells = fine_ref[pl.ds(src, step), tile * side : (tile + 1) * side, :].reshape(step * side, chans)
        queries = (jnp.dot(cells, wq_ref[...], preferred_element_type=F32) * scale).astype(BF16)
        scores = jnp.dot(queries, keys[tile], preferred_element_type=F32)
        top = jnp.max(scores, -1, keepdims=True)
        probs = jnp.exp2(scores - top).astype(BF16)
        summed = jnp.dot(probs, values[tile], preferred_element_type=F32)
        attended, weight = summed[:, :chans], summed[:, chans:]
        meansq = jnp.mean(attended * attended, -1, keepdims=True)
        mixed = cells.astype(F32) + gain * attended * lax.rsqrt(meansq + 1e-6 * weight * weight)
        out[pl.ds(dst, step), tile * side : (tile + 1) * side, :] = mixed.astype(BF16).reshape(step, side, chans)

    for (low, high), out in zip(ranges, outs):
        if high - low == step:
            for tile in range(tiles):
                some(tile, low, out, 0)
        else:

            @pl.loop(0, (high - low) // step)
            def _(i):
                for tile in range(tiles):
                    some(tile, low + i * step, out, i * step)


def attend(coverage, owner_slot, fine, w_query, gain, blocks, ranges, step):
    rows, cols, chans = fine.shape
    tiles, cover = cols // rows, coverage.shape[1]
    keys = blocks[0].shape[1]
    return pl.pallas_call(
        functools.partial(attend_kernel, ranges, step, len(blocks)),
        out_shape=[jax.ShapeDtypeStruct((high - low, cols, chans), BF16) for low, high in ranges],
        in_specs=[SMEM] * 2 + [VMEM] * 3 + [ANY] * len(blocks),
        out_specs=[VMEM] * len(ranges),
        scratch_shapes=[
            pltpu.VMEM((tiles, chans, cover * keys), BF16),
            pltpu.VMEM((tiles, cover * keys, 2 * chans), BF16),
            pltpu.SemaphoreType.DMA((tiles * cover, 1 + keys // chans)),
        ],
        compiler_params=pltpu.CompilerParams(vmem_limit_bytes=40 * 2**20),
        name="attend",
    )(coverage, owner_slot, fine, w_query, gain, *blocks)


def pair_kernel(kernels_ref, out_ref):
    chans = kernels_ref.shape[-1]
    zero = jnp.zeros((chans, chans), BF16)
    for layer in range(kernels_ref.shape[0]):
        for lower in range(2):
            for shift in range(3):
                base = (lower * 3 + shift) * 2 * chans
                for row in range(2):
                    for to in range(2):
                        tap = 2 * lower + row - to
                        out_ref[layer, base + row * chans : base + (row + 1) * chans, to * chans : (to + 1) * chans] = (
                            kernels_ref[layer, tap, shift] if 0 <= tap < 3 else zero
                        )


def paired_weights(kernels):
    layers, chans = kernels.shape[0], kernels.shape[-1]
    return pl.pallas_call(
        pair_kernel,
        out_shape=jax.ShapeDtypeStruct((layers, 12 * chans, 2 * chans), BF16),
        in_specs=[VMEM],
        out_specs=VMEM,
        compiler_params=pltpu.CompilerParams(vmem_limit_bytes=8 * 2**20),
        name="pair_weights",
    )(kernels)


def silu(x):
    half = 0.5 * x
    return half + half * jnp.tanh(half)


def conv_kernel(group, *refs):
    parts, (weight_ref, bias_ref, out_ref, state_a, state_b) = refs[:-5], refs[-5:]
    layers = weight_ref.shape[0]
    cols, chans = out_ref.shape[1:]
    column = lax.broadcasted_iota(jnp.int32, (cols, 1), 0)
    first = lax.axis_index("row") == 0
    last = lax.axis_index("row") == lax.axis_size("row") - 1

    def put(dst, pair, value):
        west = jnp.where(column == 0, 0.0, pltpu.roll(value, 1, 0))
        east = jnp.where(column == cols - 1, 0.0, pltpu.roll(value, cols - 1, 0))
        dst[0, pair] = west.astype(BF16)
        dst[1, pair] = value.astype(BF16)
        dst[2, pair] = east.astype(BF16)

    def take(ref, src, pair):
        put(state_a, pair, jnp.concatenate([ref[2 * src], ref[2 * src + 1]], -1).astype(F32))

    done = 0
    for part in parts:
        count = part.shape[0] // 2
        if count > 4:
            base = done

            @pl.loop(0, count)
            def _(i):
                take(part, i, base + i)
        else:
            for i in range(count):
                take(part, i, done + i)
        done += count

    source, target = state_a, state_b
    pairs = done
    for layer in range(layers):
        pairs -= 1
        bias = jnp.concatenate([bias_ref[layer : layer + 1, :]] * 2, -1)
        final = layer == layers - 1

        @pl.loop(0, pl.cdiv(pairs, group))
        def _(i):
            at = jnp.minimum(i * group, pairs - group)
            taps = [
                source[shift, pl.ds(at + lower, group)].reshape(group * cols, 2 * chans)
                for lower in range(2)
                for shift in range(3)
            ]
            total = jnp.dot(jnp.concatenate(taps, -1), weight_ref[layer], preferred_element_type=F32)
            value = silu(total + bias)
            for k in range(group):
                one = value[k * cols : (k + 1) * cols]
                if final:
                    rounded = one.astype(BF16)
                    out_ref[2 * (at + k)] = rounded[:, :chans]
                    out_ref[2 * (at + k) + 1] = rounded[:, chans:]
                else:
                    put(target, at + k, one)

        margin = layers - 1 - layer
        if margin:
            blank = jnp.zeros((3, cols, chans), BF16)

            @pl.when(first)
            def _():
                for row in range(margin):
                    target[:, row // 2, :, (row % 2) * chans : (row % 2 + 1) * chans] = blank

            @pl.when(last)
            def _():
                for row in range(2 * pairs - margin, 2 * pairs):
                    target[:, row // 2, :, (row % 2) * chans : (row % 2 + 1) * chans] = blank

        source, target = target, source


def convolve(parts, weights, bias, rows):
    cols, chans = parts[0].shape[1:]
    pairs = sum(part.shape[0] for part in parts) // 2
    return pl.pallas_call(
        functools.partial(conv_kernel, 8),
        out_shape=jax.ShapeDtypeStruct((rows, cols, chans), BF16),
        in_specs=[VMEM] * (len(parts) + 2),
        out_specs=VMEM,
        scratch_shapes=[pltpu.VMEM((3, pairs, cols, 2 * chans), BF16)] * 2,
        compiler_params=pltpu.CompilerParams(vmem_limit_bytes=56 * 2**20),
        name="convolve",
    )(*parts, weights, bias)


def on_device(
    fine, parent, coverage, owner_slot, w_query, w_key, w_value, norm_gain, conv_weight, conv_bias
):
    rows = fine.shape[0]
    halo = conv_weight.shape[0]
    count = lax.axis_size("row")

    blocks = gather_blocks(encode(parent[0], w_key, w_value), count)
    weights = paired_weights(conv_weight)
    over = functools.partial(attend, coverage, owner_slot, fine, w_query, norm_gain[None], blocks)
    head, tail = over(((0, halo), (rows - halo, rows)), halo)
    north = lax.ppermute(tail, "row", [(i, i + 1) for i in range(count - 1)])
    south = lax.ppermute(head, "row", [(i + 1, i) for i in range(count - 1)])
    (middle,) = over(((halo, rows - halo),), 8)
    return convolve([north, head, middle, tail, south], weights, conv_bias, rows)


def solution(mesh):
    placed = (
        P(("groups", "row"), None, None),
        P(("groups", "row"), None, None),
        P("groups", None),
        P("groups"),
        P(),
        P(),
        P(),
        P(),
        P(),
        P(),
    )
    return jax.shard_map(
        on_device,
        mesh=mesh,
        in_specs=placed,
        out_specs=P(("groups", "row"), None, None),
        check_vma=False,
    )
```

```python
import functools
import math

import jax
import jax.numpy as jnp
from jax import lax
from jax.experimental import pallas as pl
from jax.experimental.pallas import tpu as pltpu
from jax.sharding import PartitionSpec as P


BF16, F32 = jnp.bfloat16, jnp.float32
VMEM = pl.BlockSpec(memory_space=pltpu.VMEM)
SMEM = pl.BlockSpec(memory_space=pltpu.SMEM)
ANY = pl.BlockSpec(memory_space=pl.ANY)
HBM = pl.BlockSpec(memory_space=pltpu.HBM)
LARGE = 60 * 2**20
TIE = 0
STEP = 16
GROUP = 18
SUB = 4


def encode_kernel(halo, parent_hbm, wk_hbm, wv_hbm, wq_hbm, fine_hbm, out_ref, head_ref, tail_ref, *rest):
    parent_ref, wk_ref, wv_ref, wq_ref, sem = rest
    plain = (
        (parent_hbm, parent_ref),
        (wk_hbm, wk_ref),
        (wv_hbm, wv_ref),
        (wq_hbm, wq_ref),
        (fine_hbm.at[:halo], head_ref),
        (fine_hbm.at[fine_hbm.shape[0] - halo :], tail_ref),
    )
    moves = [pltpu.make_async_copy(src, dst, sem.at[i]) for i, (src, dst) in enumerate(plain)]
    for move in moves:
        move.start()
    for move in moves[:4]:
        move.wait()
    rows, chans = parent_ref.shape[0], wk_ref.shape[1]
    parent = parent_ref[...]
    keys = jnp.dot(parent, wk_ref[...], preferred_element_type=F32)
    scale = math.log2(math.e) / math.sqrt(chans)
    folded = jnp.dot(wq_ref[...], keys.T.astype(BF16), preferred_element_type=F32) * scale
    values = jnp.dot(parent, wv_ref[...], preferred_element_type=F32).astype(BF16)
    out_ref[:chans, :] = folded.astype(BF16)
    for half in range(rows // chans):
        out_ref[chans:, half * chans : (half + 1) * chans] = values[half * chans : (half + 1) * chans]
    for move in moves[4:]:
        move.wait()


def encode(parent, w_key, w_value, w_query, fine, halo):
    rows, chans = parent.shape[0], w_key.shape[1]
    edge = jax.ShapeDtypeStruct((halo,) + fine.shape[1:], BF16)
    return pl.pallas_call(
        functools.partial(encode_kernel, halo),
        out_shape=[jax.ShapeDtypeStruct((2 * chans, rows), BF16), edge, edge],
        in_specs=[HBM] * 5,
        out_specs=[VMEM] * 3,
        scratch_shapes=[pltpu.VMEM(a.shape, a.dtype) for a in (parent, w_key, w_value, w_query)]
        + [pltpu.SemaphoreType.DMA((6,))],
        compiler_params=pltpu.CompilerParams(vmem_limit_bytes=LARGE),
        name="encode",
    )(parent, w_key, w_value, w_query, fine)


def ring_shape(count):
    per_chip = 2 if count % 2 == 0 else 1
    return per_chip, count // per_chip


def ring_place(chip, chips):
    half = lax.div(chip, 2)
    return jnp.where(lax.rem(chip, 2) == 0, half, chips - 1 - half)


def gather_blocks(block, count, north, south):
    per_chip, chips = ring_shape(count)
    order = list(range(0, chips, 2)) + list(range(1, chips, 2))[::-1]

    def step(array, shift):
        pairs = [
            (order[at] * per_chip + core, order[(at + shift) % chips] * per_chip + core)
            for at in range(chips)
            for core in range(per_chip)
        ]
        return lax.ppermute(array, "row", pairs)

    held = {0: block}
    ahead = behind = block
    up, down = chips // 2, (chips - 1) // 2
    for hop in range(1, up + 1):
        ahead = step(ahead, 1)
        held[chips - hop] = ahead
        if hop <= down:
            behind = step(behind, -1)
            held[hop] = behind
        if hop == TIE:
            ahead, behind, north, south = lax.optimization_barrier((ahead, behind, north, south))
            held[chips - hop], held[hop] = ahead, behind
    own = [held[offset] for offset in range(chips)]
    if per_chip == 1:
        return own, north, south
    partner = [(i, i ^ 1) for i in range(count)]
    return own + [lax.ppermute(array, "row", partner) for array in own], north, south


def main_kernel(
    count, step, coverage_ref, owner_ref, fine_hbm, north_hbm, south_hbm, gain_hbm, kernel_hbm, bias_hbm, *rest
):
    blocks, out_hbm, rest = rest[:count], rest[count], rest[count + 1 :]
    cells, mixed, keys, values, scores, tops, gain_v, kernels, weight, bias_v, state_a, state_b = rest[:12]
    rows_f32, out, sem_kv, sem = rest[12:]
    halo, own = north_hbm.shape[0], fine_hbm.shape[0]
    cols, chans = cells.shape[1:]
    half = cols // 2
    tiles = coverage_ref.shape[0] // count
    cover = coverage_ref.shape[1]
    kv_rows = blocks[0].shape[1]
    layers = weight.shape[0]
    wide = cols // tiles
    per_chip, chips = ring_shape(count)
    position = lax.axis_index("row")
    home = ring_place(lax.div(position, per_chip), chips)
    core = lax.rem(position, per_chip)
    first, last = position == 0, position == count - 1

    plain = [
        (kernel_hbm, kernels),
        (fine_hbm, cells.at[halo : halo + own]),
        (gain_hbm, gain_v),
        (north_hbm, cells.at[0:halo]),
        (south_hbm, cells.at[halo + own :]),
        (bias_hbm, bias_v),
    ]
    moves = [pltpu.make_async_copy(src, dst, sem.at[i]) for i, (src, dst) in enumerate(plain)]
    for move in moves[:3]:
        move.start()
    block_moves = []
    for at, ref in enumerate(blocks):
        block_moves.append(pltpu.make_async_copy(ref.at[0:chans], keys.at[at], sem_kv.at[at, 0]))
        for part in range(kv_rows // chans):
            block_moves.append(
                pltpu.make_async_copy(
                    ref.at[chans : 2 * chans, part * chans : (part + 1) * chans],
                    values.at[at, part * chans : (part + 1) * chans, 0:chans],
                    sem_kv.at[at, 1 + part],
                )
            )
    for move in block_moves + moves[3:]:
        move.start()
    values[:, :, chans:] = jnp.ones(values.shape[:2] + (values.shape[2] - chans,), BF16)

    def picks(level, tile):
        line = jnp.minimum(jnp.maximum(position + level, 0), count - 1)
        out = []
        for j in range(cover):
            slot = owner_ref[coverage_ref[line * tiles + tile, j]]
            offset = ring_place(lax.div(slot, per_chip), chips) - home
            offset = jnp.where(offset < 0, offset + chips, offset)
            out.append(jnp.where(lax.rem(slot, per_chip) == core, 0, chips) + offset)
        return out

    chosen = {(level, tile): picks(level, tile) for level in (0, -1, 1) for tile in range(tiles)}

    moves[0].wait()
    zero = jnp.zeros((chans, chans), BF16)

    @pl.loop(0, layers)
    def _(layer):
        for tap in range(3):
            west, centre, east = (kernels[layer, tap, shift].astype(F32) for shift in range(3))
            outer = west + east
            terms = (0.5 * west, 0.25 * (outer + centre), 0.25 * (outer - centre), 0.5 * east)
            for term, value in enumerate(terms):
                value = value.astype(BF16)
                for to in range(2):
                    row = tap + to
                    weight[layer, term, row * chans : (row + 1) * chans, to * chans : (to + 1) * chans] = value
        for term in range(4):
            weight[layer, term, 3 * chans :, :chans] = zero
            weight[layer, term, :chans, chans:] = zero

    for move in moves[1:3] + block_moves:
        move.wait()
    gain = gain_v[...]

    def score(slot, row, size, level, tile):
        amount = size * wide
        part = cells[pl.ds(row, size), tile * wide : (tile + 1) * wide, :].reshape(amount, chans)
        top = None
        for j, which in enumerate(chosen[level, tile]):
            found = jnp.dot(part, keys[which], preferred_element_type=F32)
            scores[slot, :amount, j * kv_rows : (j + 1) * kv_rows] = found
            for lane in range(0, kv_rows, 128):
                piece = found[:, lane : lane + 128]
                top = piece if top is None else jnp.maximum(top, piece)
        tops[slot, :amount] = jnp.broadcast_to(jnp.max(top, -1, keepdims=True), (amount, 128))

    def mix(slot, row, size, level, tile):
        amount = size * wide
        top = tops[slot, :amount]
        probs = [
            jnp.exp2(scores[slot, :amount, lane : lane + 128] - top).astype(BF16)
            for lane in range(0, cover * kv_rows, 128)
        ]
        covered = jnp.concatenate([values[which] for which in chosen[level, tile]], 0)
        summed = jnp.dot(jnp.concatenate(probs, -1), covered, preferred_element_type=F32)
        attended, mass = summed[:, :chans], summed[:, chans:]
        meansq = jnp.mean(attended * attended, -1, keepdims=True)
        part = cells[pl.ds(row, size), tile * wide : (tile + 1) * wide, :].reshape(amount, chans)
        total = part.astype(F32) + gain * attended * lax.rsqrt(meansq + 1e-6 * mass * mass)
        mixed[pl.ds(row, size), tile * wide : (tile + 1) * wide, :] = total.reshape(size, wide, chans)

    score(0, halo, step, 0, 0)

    @pl.loop(0, own // step - 1)
    def _(i):
        row = halo + i * step
        for tile in range(tiles):
            ahead = (tile + 1) % tiles
            score(ahead % 2, row + (step if ahead == 0 else 0), step, 0, ahead)
            mix(tile % 2, row, step, 0, tile)

    for move in moves[3:]:
        move.wait()
    pieces = [(halo + own - step, step, 0, tile) for tile in range(tiles)]
    pieces += [(0, halo, -1, tile) for tile in range(tiles)]
    pieces += [(halo + own, halo, 1, tile) for tile in range(tiles)]
    for at, piece in enumerate(pieces):
        if at + 1 < len(pieces):
            score((at + 1) % 2, *pieces[at + 1])
        mix(at % 2, *piece)

    @pl.when(first)
    def _():
        mixed[:halo] = jnp.zeros((halo, cols, chans), F32)

    @pl.when(last)
    def _():
        mixed[halo + own :] = jnp.zeros((halo, cols, chans), F32)

    def put(dst, pair, amount, even, odd):
        column = lax.rem(lax.broadcasted_iota(jnp.int32, (amount * half, 1), 0), half)
        before = jnp.where(column == 0, 0.0, pltpu.roll(odd, 1, 0))
        after = jnp.where(column == half - 1, 0.0, pltpu.roll(even, amount * half - 1, 0))
        for term, value in enumerate((before - odd, even + odd, odd - even, even - after)):
            dst[term, pl.ds(pair, amount)] = value.astype(BF16).reshape(amount, half, 2 * chans)

    pairs = (own + 2 * halo) // 2

    batch = 4 if pairs % 4 == 0 else 1

    @pl.loop(0, pairs // batch)
    def _(i):
        for pair in range(batch):
            even, odd = (
                jnp.concatenate(
                    [mixed.at[2 * (i * batch + pair) + k][pl.ds(side, half, stride=2), :] for k in range(2)], -1
                )
                for side in range(2)
            )
            put(state_a, i * batch + pair, 1, even, odd)

    source, target = state_a, state_b
    for layer in range(layers):
        pairs -= 1
        group = min(range(GROUP // 2, GROUP + 1), key=lambda size: (-(-pairs // size) * size, -size))
        final = layer == layers - 1
        bias = 0.5 * jnp.concatenate([bias_v[layer : layer + 1, :]] * 2, -1)

        def convolve(at, amount, spare):
            terms = []
            for term in range(4):
                taps = [source[term, pl.ds(at + lower, amount)].reshape(amount * half, 2 * chans) for lower in range(2)]
                terms.append(jnp.dot(jnp.concatenate(taps, -1), weight[layer, term], preferred_element_type=F32))
            centre = terms[1] + bias
            even = centre + terms[2] + terms[0]
            odd = centre - terms[2] - terms[3]
            even = even + even * jnp.tanh(even)
            odd = odd + odd * jnp.tanh(odd)
            if not final:
                put(target, at, amount, even, odd)
                return
            for k in range(amount):
                for side in range(2):
                    one = rows_f32.at[spare + 2 * k + side]
                    one[pl.ds(0, half, stride=2), :] = even[k * half : (k + 1) * half, side * chans : (side + 1) * chans]
                    one[pl.ds(1, half, stride=2), :] = odd[k * half : (k + 1) * half, side * chans : (side + 1) * chans]
            out[pl.ds(2 * at, 2 * amount)] = rows_f32[spare : spare + 2 * amount].astype(BF16)

        @pl.loop(0, pl.cdiv(pairs, group))
        def _(i):
            start = jnp.minimum(i * group, pairs - group)
            subs = -(-group // SUB)
            for sub in range(subs):
                low, high = sub * group // subs, (sub + 1) * group // subs
                convolve(start + low, high - low, 2 * low)

        margin = layers - 1 - layer
        if margin:
            blank = jnp.zeros((4, half, chans), BF16)

            @pl.when(first)
            def _():
                for row in range(margin):
                    target[:, row // 2, :, (row % 2) * chans : (row % 2 + 1) * chans] = blank

            @pl.when(last)
            def _():
                for row in range(2 * pairs - margin, 2 * pairs):
                    target[:, row // 2, :, (row % 2) * chans : (row % 2 + 1) * chans] = blank

        source, target = target, source
    move = pltpu.make_async_copy(out, out_hbm, sem.at[len(plain)])
    move.start()
    move.wait()


def attend_and_convolve(coverage, owner_slot, fine, north, south, gain, kernels, bias, blocks):
    own, cols, chans = fine.shape
    halo, count, cover = north.shape[0], len(blocks), coverage.shape[1]
    tiles = coverage.shape[0] // count
    kv_rows = blocks[0].shape[1]
    amount = STEP * cols // tiles
    total = own + 2 * halo
    state = pltpu.VMEM((4, total // 2, cols // 2, 2 * chans), BF16)
    return pl.pallas_call(
        functools.partial(main_kernel, count, STEP),
        out_shape=jax.ShapeDtypeStruct(fine.shape, BF16),
        in_specs=[SMEM] * 2 + [HBM] * (6 + count),
        out_specs=HBM,
        scratch_shapes=[
            pltpu.VMEM((total, cols, chans), BF16),
            pltpu.VMEM((total, cols, chans), F32),
            pltpu.VMEM((count, chans, kv_rows), BF16),
            pltpu.VMEM((count, kv_rows, 2 * chans), BF16),
            pltpu.VMEM((2, amount, cover * kv_rows), F32),
            pltpu.VMEM((2, amount, 128), F32),
            pltpu.VMEM(gain.shape, F32),
            pltpu.VMEM(kernels.shape, BF16),
            pltpu.VMEM((kernels.shape[0], 4, 4 * chans, 2 * chans), BF16),
            pltpu.VMEM(bias.shape, F32),
            state,
            state,
            pltpu.VMEM((2 * GROUP, cols, chans), F32),
            pltpu.VMEM(fine.shape, BF16),
            pltpu.SemaphoreType.DMA((count, 1 + kv_rows // chans)),
            pltpu.SemaphoreType.DMA((7,)),
        ],
        compiler_params=pltpu.CompilerParams(vmem_limit_bytes=LARGE),
        name="attend_and_convolve",
    )(coverage, owner_slot, fine, north, south, gain, kernels, bias, *blocks)


def on_device(
    fine, parent, coverage, owner_slot, w_query, w_key, w_value, norm_gain, conv_weight, conv_bias
):
    count = lax.axis_size("row")
    block, head, tail = encode(parent[0], w_key, w_value, w_query, fine, conv_weight.shape[0])
    north = lax.ppermute(tail, "row", [(i, i + 1) for i in range(count - 1)])
    south = lax.ppermute(head, "row", [(i + 1, i) for i in range(count - 1)])
    blocks, north, south = gather_blocks(block, count, north, south)
    return attend_and_convolve(
        coverage, owner_slot, fine, north, south, norm_gain[None], conv_weight, conv_bias, blocks
    )


def solution(mesh):
    placed = (
        P(("groups", "row"), None, None),
        P(("groups", "row"), None, None),
        P("groups", None),
        P("groups"),
        P(),
        P(),
        P(),
        P(),
        P(),
        P(),
    )
    return jax.shard_map(
        on_device,
        mesh=mesh,
        in_specs=placed,
        out_specs=P(("groups", "row"), None, None),
        check_vma=False,
    )
```

```python
import functools
import math

import jax
import jax.numpy as jnp
from jax import lax
from jax.experimental import pallas as pl
from jax.experimental.pallas import tpu as pltpu
from jax.sharding import PartitionSpec as P


BF16, F32 = jnp.bfloat16, jnp.float32
VMEM = pl.BlockSpec(memory_space=pltpu.VMEM)
SMEM = pl.BlockSpec(memory_space=pltpu.SMEM)
ANY = pl.BlockSpec(memory_space=pl.ANY)
HBM = pl.BlockSpec(memory_space=pltpu.HBM)
LARGE = 60 * 2**20
STEP = 16
GROUP = 18
SUB = 4


def encode_kernel(halo, parent_hbm, wk_hbm, wv_hbm, wq_hbm, fine_hbm, out_ref, inner_ref, outer_ref, *rest):
    parent_ref, wk_ref, wv_ref, wq_ref, sem = rest
    own = fine_hbm.shape[0]
    even = lax.rem(lax.axis_index("row"), 2) == 0
    plain = (
        (parent_hbm, parent_ref),
        (wk_hbm, wk_ref),
        (wv_hbm, wv_ref),
        (wq_hbm, wq_ref),
        (fine_hbm.at[pl.ds(jnp.where(even, own - halo, 0), halo)], inner_ref),
        (fine_hbm.at[pl.ds(jnp.where(even, 0, own - halo), halo)], outer_ref),
    )
    moves = [pltpu.make_async_copy(src, dst, sem.at[i]) for i, (src, dst) in enumerate(plain)]
    for move in moves:
        move.start()
    for move in moves[:4]:
        move.wait()
    rows, chans = parent_ref.shape[0], wk_ref.shape[1]
    parent = parent_ref[...]
    keys = jnp.dot(parent, wk_ref[...], preferred_element_type=F32)
    scale = math.log2(math.e) / math.sqrt(chans)
    folded = jnp.dot(wq_ref[...], keys.T.astype(BF16), preferred_element_type=F32) * scale
    values = jnp.dot(parent, wv_ref[...], preferred_element_type=F32).astype(BF16)
    out_ref[:chans, :] = folded.astype(BF16)
    for half in range(rows // chans):
        out_ref[chans:, half * chans : (half + 1) * chans] = values[half * chans : (half + 1) * chans]
    for move in moves[4:]:
        move.wait()


def encode(parent, w_key, w_value, w_query, fine, halo):
    rows, chans = parent.shape[0], w_key.shape[1]
    edge = jax.ShapeDtypeStruct((halo,) + fine.shape[1:], BF16)
    return pl.pallas_call(
        functools.partial(encode_kernel, halo),
        out_shape=[jax.ShapeDtypeStruct((2 * chans, rows), BF16), edge, edge],
        in_specs=[HBM] * 5,
        out_specs=[VMEM] * 3,
        scratch_shapes=[pltpu.VMEM(a.shape, a.dtype) for a in (parent, w_key, w_value, w_query)]
        + [pltpu.SemaphoreType.DMA((6,))],
        compiler_params=pltpu.CompilerParams(vmem_limit_bytes=LARGE),
        name="encode",
    )(parent, w_key, w_value, w_query, fine)


def ring_shape(count):
    per_chip = 2 if count % 2 == 0 else 1
    return per_chip, count // per_chip


def ring_place(chip, chips):
    half = lax.div(chip, 2)
    return jnp.where(lax.rem(chip, 2) == 0, half, chips - 1 - half)


def gather_blocks(block, count):
    per_chip, chips = ring_shape(count)
    order = list(range(0, chips, 2)) + list(range(1, chips, 2))[::-1]

    def step(array, shift):
        pairs = [
            (order[at] * per_chip + core, order[(at + shift) % chips] * per_chip + core)
            for at in range(chips)
            for core in range(per_chip)
        ]
        return lax.ppermute(array, "row", pairs)

    held = {0: block}
    ahead = behind = block
    up, down = chips // 2, (chips - 1) // 2
    for hop in range(1, up + 1):
        ahead = step(ahead, 1)
        held[chips - hop] = ahead
        if hop <= down:
            behind = step(behind, -1)
            held[hop] = behind
    own = [held[offset] for offset in range(chips)]
    if per_chip == 1:
        return own
    partner = [(i, i ^ 1) for i in range(count)]
    return own + [lax.ppermute(array, "row", partner) for array in own]


def main_kernel(
    count, step, coverage_ref, owner_ref, fine_hbm, inner_hbm, outer_hbm, gain_hbm, kernel_hbm, bias_hbm, *rest
):
    blocks, out_hbm, rest = rest[:count], rest[count], rest[count + 1 :]
    cells, mixed, keys, values, scores, tops, gain_v, kernels, weight, bias_v, state_a, state_b = rest[:12]
    rows_f32, out, sem_kv, sem, sem_out = rest[12:]
    halo, own = inner_hbm.shape[0], fine_hbm.shape[0]
    cols, chans = cells.shape[1:]
    half = cols // 2
    tiles = coverage_ref.shape[0] // count
    cover = coverage_ref.shape[1]
    kv_rows = blocks[0].shape[1]
    layers = weight.shape[0]
    wide = cols // tiles
    per_chip, chips = ring_shape(count)
    position = lax.axis_index("row")
    home = ring_place(lax.div(position, per_chip), chips)
    core = lax.rem(position, per_chip)
    first, last = position == 0, position == count - 1
    even = lax.rem(position, 2) == 0

    plain = [
        (kernel_hbm, kernels),
        (fine_hbm, cells.at[halo : halo + own]),
        (gain_hbm, gain_v),
        (inner_hbm, cells.at[pl.ds(jnp.where(even, halo + own, 0), halo)]),
        (outer_hbm, cells.at[pl.ds(jnp.where(even, 0, halo + own), halo)]),
        (bias_hbm, bias_v),
    ]
    moves = [pltpu.make_async_copy(src, dst, sem.at[i]) for i, (src, dst) in enumerate(plain)]
    for move in moves[:3]:
        move.start()
    block_moves = []
    for at, ref in enumerate(blocks):
        block_moves.append(pltpu.make_async_copy(ref.at[0:chans], keys.at[at], sem_kv.at[at, 0]))
        for part in range(kv_rows // chans):
            block_moves.append(
                pltpu.make_async_copy(
                    ref.at[chans : 2 * chans, part * chans : (part + 1) * chans],
                    values.at[at, part * chans : (part + 1) * chans, 0:chans],
                    sem_kv.at[at, 1 + part],
                )
            )
    for move in block_moves + moves[3:]:
        move.start()
    values[:, :, chans:] = jnp.ones(values.shape[:2] + (values.shape[2] - chans,), BF16)

    def picks(level, tile):
        line = jnp.minimum(jnp.maximum(position + level, 0), count - 1)
        out = []
        for j in range(cover):
            slot = owner_ref[coverage_ref[line * tiles + tile, j]]
            offset = ring_place(lax.div(slot, per_chip), chips) - home
            offset = jnp.where(offset < 0, offset + chips, offset)
            out.append(jnp.where(lax.rem(slot, per_chip) == core, 0, chips) + offset)
        return out

    chosen = {(level, tile): picks(level, tile) for level in (0, -1, 1) for tile in range(tiles)}

    moves[0].wait()
    zero = jnp.zeros((chans, chans), BF16)

    @pl.loop(0, layers)
    def _(layer):
        for tap in range(3):
            west, centre, east = (kernels[layer, tap, shift].astype(F32) for shift in range(3))
            outer = west + east
            terms = (0.5 * west, 0.25 * (outer + centre), 0.25 * (outer - centre), 0.5 * east)
            for term, value in enumerate(terms):
                value = value.astype(BF16)
                for to in range(2):
                    row = tap + to
                    weight[layer, term, row * chans : (row + 1) * chans, to * chans : (to + 1) * chans] = value
        for term in range(4):
            weight[layer, term, 3 * chans :, :chans] = zero
            weight[layer, term, :chans, chans:] = zero

    for move in moves[1:3] + block_moves:
        move.wait()
    gain = gain_v[...]

    def score(slot, row, size, level, tile):
        amount = size * wide
        part = cells[pl.ds(row, size), tile * wide : (tile + 1) * wide, :].reshape(amount, chans)
        top = None
        for j, which in enumerate(chosen[level, tile]):
            found = jnp.dot(part, keys[which], preferred_element_type=F32)
            scores[slot, :amount, j * kv_rows : (j + 1) * kv_rows] = found
            for lane in range(0, kv_rows, 128):
                piece = found[:, lane : lane + 128]
                top = piece if top is None else jnp.maximum(top, piece)
        tops[slot, :amount] = jnp.broadcast_to(jnp.max(top, -1, keepdims=True), (amount, 128))

    def mix(slot, row, size, level, tile):
        amount = size * wide
        top = tops[slot, :amount]
        probs = [
            jnp.exp2(scores[slot, :amount, lane : lane + 128] - top).astype(BF16)
            for lane in range(0, cover * kv_rows, 128)
        ]
        covered = jnp.concatenate([values[which] for which in chosen[level, tile]], 0)
        summed = jnp.dot(jnp.concatenate(probs, -1), covered, preferred_element_type=F32)
        attended, mass = summed[:, :chans], summed[:, chans:]
        meansq = jnp.mean(attended * attended, -1, keepdims=True)
        part = cells[pl.ds(row, size), tile * wide : (tile + 1) * wide, :].reshape(amount, chans)
        total = part.astype(F32) + gain * attended * lax.rsqrt(meansq + 1e-6 * mass * mass)
        mixed[pl.ds(row, size), tile * wide : (tile + 1) * wide, :] = total.reshape(size, wide, chans)

    score(0, halo, step, 0, 0)

    @pl.loop(0, own // step - 1)
    def _(i):
        row = halo + i * step
        for tile in range(tiles):
            ahead = (tile + 1) % tiles
            score(ahead % 2, row + (step if ahead == 0 else 0), step, 0, ahead)
            mix(tile % 2, row, step, 0, tile)

    for move in moves[3:]:
        move.wait()
    pieces = [(halo + own - step, step, 0, tile) for tile in range(tiles)]
    pieces += [(0, halo, -1, tile) for tile in range(tiles)]
    pieces += [(halo + own, halo, 1, tile) for tile in range(tiles)]
    for at, piece in enumerate(pieces):
        if at + 1 < len(pieces):
            score((at + 1) % 2, *pieces[at + 1])
        mix(at % 2, *piece)

    @pl.when(first)
    def _():
        mixed[:halo] = jnp.zeros((halo, cols, chans), F32)

    @pl.when(last)
    def _():
        mixed[halo + own :] = jnp.zeros((halo, cols, chans), F32)

    def put(dst, pair, amount, even, odd):
        column = lax.rem(lax.broadcasted_iota(jnp.int32, (amount * half, 1), 0), half)
        before = jnp.where(column == 0, 0.0, pltpu.roll(odd, 1, 0))
        after = jnp.where(column == half - 1, 0.0, pltpu.roll(even, amount * half - 1, 0))
        for term, value in enumerate((before - odd, even + odd, odd - even, even - after)):
            dst[term, pl.ds(pair, amount)] = value.astype(BF16).reshape(amount, half, 2 * chans)

    pairs = (own + 2 * halo) // 2

    batch = 4 if pairs % 4 == 0 else 1

    @pl.loop(0, pairs // batch)
    def _(i):
        for pair in range(batch):
            even, odd = (
                jnp.concatenate(
                    [mixed.at[2 * (i * batch + pair) + k][pl.ds(side, half, stride=2), :] for k in range(2)], -1
                )
                for side in range(2)
            )
            put(state_a, i * batch + pair, 1, even, odd)

    source, target = state_a, state_b
    for layer in range(layers):
        pairs -= 1
        group = min(range(GROUP // 2, GROUP + 1), key=lambda size: (-(-pairs // size) * size, -size))
        final = layer == layers - 1
        bias = 0.5 * jnp.concatenate([bias_v[layer : layer + 1, :]] * 2, -1)

        def convolve(at, amount, spare):
            terms = []
            for term in range(4):
                taps = [source[term, pl.ds(at + lower, amount)].reshape(amount * half, 2 * chans) for lower in range(2)]
                terms.append(jnp.dot(jnp.concatenate(taps, -1), weight[layer, term], preferred_element_type=F32))
            centre = terms[1] + bias
            even = centre + terms[2] + terms[0]
            odd = centre - terms[2] - terms[3]
            even = even + even * jnp.tanh(even)
            odd = odd + odd * jnp.tanh(odd)
            if not final:
                put(target, at, amount, even, odd)
                return
            for k in range(amount):
                for side in range(2):
                    one = rows_f32.at[spare + 2 * k + side]
                    one[pl.ds(0, half, stride=2), :] = even[k * half : (k + 1) * half, side * chans : (side + 1) * chans]
                    one[pl.ds(1, half, stride=2), :] = odd[k * half : (k + 1) * half, side * chans : (side + 1) * chans]
            out[pl.ds(2 * at, 2 * amount)] = rows_f32[spare : spare + 2 * amount].astype(BF16)

        @pl.loop(0, pl.cdiv(pairs, group))
        def _(i):
            start = jnp.minimum(i * group, pairs - group)
            subs = -(-group // SUB)
            for sub in range(subs):
                low, high = sub * group // subs, (sub + 1) * group // subs
                convolve(start + low, high - low, 2 * low)
            if final and pairs % group == 0:
                part = pl.ds(2 * start, 2 * group)
                pltpu.make_async_copy(out.at[part], out_hbm.at[part], sem_out.at[i]).start()

        margin = layers - 1 - layer
        if margin:
            blank = jnp.zeros((4, half, chans), BF16)

            @pl.when(first)
            def _():
                for row in range(margin):
                    target[:, row // 2, :, (row % 2) * chans : (row % 2 + 1) * chans] = blank

            @pl.when(last)
            def _():
                for row in range(2 * pairs - margin, 2 * pairs):
                    target[:, row // 2, :, (row % 2) * chans : (row % 2 + 1) * chans] = blank

        source, target = target, source
    if pairs % group == 0:
        for i in range(pairs // group):
            part = slice(2 * i * group, 2 * (i + 1) * group)
            pltpu.make_async_copy(out.at[part], out_hbm.at[part], sem_out.at[i]).wait()
    else:
        move = pltpu.make_async_copy(out, out_hbm, sem_out.at[0])
        move.start()
        move.wait()


def attend_and_convolve(coverage, owner_slot, fine, inner, outer, gain, kernels, bias, blocks):
    own, cols, chans = fine.shape
    halo, count, cover = inner.shape[0], len(blocks), coverage.shape[1]
    tiles = coverage.shape[0] // count
    kv_rows = blocks[0].shape[1]
    amount = STEP * cols // tiles
    total = own + 2 * halo
    state = pltpu.VMEM((4, total // 2, cols // 2, 2 * chans), BF16)
    return pl.pallas_call(
        functools.partial(main_kernel, count, STEP),
        out_shape=jax.ShapeDtypeStruct(fine.shape, BF16),
        in_specs=[SMEM] * 2 + [HBM] * (6 + count),
        out_specs=HBM,
        scratch_shapes=[
            pltpu.VMEM((total, cols, chans), BF16),
            pltpu.VMEM((total, cols, chans), F32),
            pltpu.VMEM((count, chans, kv_rows), BF16),
            pltpu.VMEM((count, kv_rows, 2 * chans), BF16),
            pltpu.VMEM((2, amount, cover * kv_rows), F32),
            pltpu.VMEM((2, amount, 128), F32),
            pltpu.VMEM(gain.shape, F32),
            pltpu.VMEM(kernels.shape, BF16),
            pltpu.VMEM((kernels.shape[0], 4, 4 * chans, 2 * chans), BF16),
            pltpu.VMEM(bias.shape, F32),
            state,
            state,
            pltpu.VMEM((2 * GROUP, cols, chans), F32),
            pltpu.VMEM(fine.shape, BF16),
            pltpu.SemaphoreType.DMA((count, 1 + kv_rows // chans)),
            pltpu.SemaphoreType.DMA((6,)),
            pltpu.SemaphoreType.DMA((own // 2,)),
        ],
        compiler_params=pltpu.CompilerParams(vmem_limit_bytes=LARGE),
        name="attend_and_convolve",
    )(coverage, owner_slot, fine, inner, outer, gain, kernels, bias, *blocks)


def on_device(
    fine, parent, coverage, owner_slot, w_query, w_key, w_value, norm_gain, conv_weight, conv_bias
):
    count = lax.axis_size("row")
    block, inner, outer = encode(parent[0], w_key, w_value, w_query, fine, conv_weight.shape[0])
    swap = lambda array, low: lax.ppermute(
        array, "row", [pair for i in range(low, count - 1, 2) for pair in ((i, i + 1), (i + 1, i))]
    )
    inner, outer = swap(inner, 0), swap(outer, 1)
    blocks = gather_blocks(block, count)
    return attend_and_convolve(
        coverage, owner_slot, fine, inner, outer, norm_gain[None], conv_weight, conv_bias, blocks
    )


def solution(mesh):
    placed = (
        P(("groups", "row"), None, None),
        P(("groups", "row"), None, None),
        P("groups", None),
        P("groups"),
        P(),
        P(),
        P(),
        P(),
        P(),
        P(),
    )
    return jax.shard_map(
        on_device,
        mesh=mesh,
        in_specs=placed,
        out_specs=P(("groups", "row"), None, None),
        check_vma=False,
    )
```

```python
import functools
import math

import jax
import jax.numpy as jnp
from jax import lax
from jax.experimental import pallas as pl
from jax.experimental.pallas import tpu as pltpu
from jax.sharding import PartitionSpec as P


BF16, F32 = jnp.bfloat16, jnp.float32
VMEM = pl.BlockSpec(memory_space=pltpu.VMEM)
SMEM = pl.BlockSpec(memory_space=pltpu.SMEM)
ANY = pl.BlockSpec(memory_space=pl.ANY)
HBM = pl.BlockSpec(memory_space=pltpu.HBM)
LARGE = 60 * 2**20
STEP = 16
GROUP = 18
SUB = 4


def encode_kernel(halo, parent_hbm, wk_hbm, wv_hbm, wq_hbm, fine_hbm, out_ref, inner_ref, outer_ref, *rest):
    parent_ref, wk_ref, wv_ref, wq_ref, sem = rest
    own = fine_hbm.shape[0]
    even = lax.rem(lax.axis_index("row"), 2) == 0
    plain = (
        (parent_hbm, parent_ref),
        (wk_hbm, wk_ref),
        (wv_hbm, wv_ref),
        (wq_hbm, wq_ref),
        (fine_hbm.at[pl.ds(jnp.where(even, own - halo, 0), halo)], inner_ref),
        (fine_hbm.at[pl.ds(jnp.where(even, 0, own - halo), halo)], outer_ref),
    )
    moves = [pltpu.make_async_copy(src, dst, sem.at[i]) for i, (src, dst) in enumerate(plain)]
    for move in moves:
        move.start()
    for move in moves[:4]:
        move.wait()
    rows, chans = parent_ref.shape[0], wk_ref.shape[1]
    parent = parent_ref[...]
    keys = jnp.dot(parent, wk_ref[...], preferred_element_type=F32)
    scale = math.log2(math.e) / math.sqrt(chans)
    folded = jnp.dot(wq_ref[...], keys.T.astype(BF16), preferred_element_type=F32) * scale
    values = jnp.dot(parent, wv_ref[...], preferred_element_type=F32).astype(BF16)
    out_ref[:chans, :] = folded.astype(BF16)
    for half in range(rows // chans):
        out_ref[chans:, half * chans : (half + 1) * chans] = values[half * chans : (half + 1) * chans]
    for move in moves[4:]:
        move.wait()


def encode(parent, w_key, w_value, w_query, fine, halo):
    rows, chans = parent.shape[0], w_key.shape[1]
    edge = jax.ShapeDtypeStruct((halo,) + fine.shape[1:], BF16)
    return pl.pallas_call(
        functools.partial(encode_kernel, halo),
        out_shape=[jax.ShapeDtypeStruct((2 * chans, rows), BF16), edge, edge],
        in_specs=[HBM] * 5,
        out_specs=[VMEM] * 3,
        scratch_shapes=[pltpu.VMEM(a.shape, a.dtype) for a in (parent, w_key, w_value, w_query)]
        + [pltpu.SemaphoreType.DMA((6,))],
        compiler_params=pltpu.CompilerParams(vmem_limit_bytes=LARGE),
        name="encode",
    )(parent, w_key, w_value, w_query, fine)


def ring_shape(count):
    per_chip = 2 if count % 2 == 0 else 1
    return per_chip, count // per_chip


def ring_place(chip, chips):
    half = lax.div(chip, 2)
    return jnp.where(lax.rem(chip, 2) == 0, half, chips - 1 - half)


def gather_blocks(block, count):
    per_chip, chips = ring_shape(count)
    order = list(range(0, chips, 2)) + list(range(1, chips, 2))[::-1]

    def step(array, shift):
        pairs = [
            (order[at] * per_chip + core, order[(at + shift) % chips] * per_chip + core)
            for at in range(chips)
            for core in range(per_chip)
        ]
        return lax.ppermute(array, "row", pairs)

    held = {0: block}
    ahead = behind = block
    up, down = chips // 2, (chips - 1) // 2
    for hop in range(1, up + 1):
        ahead = step(ahead, 1)
        held[chips - hop] = ahead
        if hop <= down:
            behind = step(behind, -1)
            held[hop] = behind
    own = [held[offset] for offset in range(chips)]
    if per_chip == 1:
        return own
    partner = [(i, i ^ 1) for i in range(count)]
    others = []
    for array in own:
        others.append(lax.ppermute(array, "row", partner))
    return own + others


def main_kernel(
    count, step, coverage_ref, owner_ref, fine_hbm, inner_hbm, outer_hbm, gain_hbm, kernel_hbm, bias_hbm, *rest
):
    blocks, out_hbm, rest = rest[:count], rest[count], rest[count + 1 :]
    cells, mixed, keys, values, scores, tops, gain_v, kernels, weight, bias_v, state_a, state_b = rest[:12]
    rows_f32, out, sem_kv, sem, sem_out = rest[12:]
    halo, own = inner_hbm.shape[0], fine_hbm.shape[0]
    cols, chans = cells.shape[1:]
    half = cols // 2
    tiles = coverage_ref.shape[0] // count
    cover = coverage_ref.shape[1]
    kv_rows = blocks[0].shape[1]
    layers = weight.shape[0]
    wide = cols // tiles
    per_chip, chips = ring_shape(count)
    position = lax.axis_index("row")
    home = ring_place(lax.div(position, per_chip), chips)
    core = lax.rem(position, per_chip)
    first, last = position == 0, position == count - 1
    even = lax.rem(position, 2) == 0

    plain = [
        (kernel_hbm, kernels),
        (fine_hbm, cells.at[halo : halo + own]),
        (gain_hbm, gain_v),
        (inner_hbm, cells.at[pl.ds(jnp.where(even, halo + own, 0), halo)]),
        (outer_hbm, cells.at[pl.ds(jnp.where(even, 0, halo + own), halo)]),
        (bias_hbm, bias_v),
    ]
    moves = [pltpu.make_async_copy(src, dst, sem.at[i]) for i, (src, dst) in enumerate(plain)]
    for move in moves[:3]:
        move.start()
    block_moves = []
    for at, ref in enumerate(blocks):
        block_moves.append(pltpu.make_async_copy(ref.at[0:chans], keys.at[at], sem_kv.at[at, 0]))
        for part in range(kv_rows // chans):
            block_moves.append(
                pltpu.make_async_copy(
                    ref.at[chans : 2 * chans, part * chans : (part + 1) * chans],
                    values.at[at, part * chans : (part + 1) * chans, 0:chans],
                    sem_kv.at[at, 1 + part],
                )
            )
    for move in block_moves + moves[3:]:
        move.start()
    values[:, :, chans:] = jnp.ones(values.shape[:2] + (values.shape[2] - chans,), BF16)

    def picks(level, tile):
        line = jnp.minimum(jnp.maximum(position + level, 0), count - 1)
        out = []
        for j in range(cover):
            slot = owner_ref[coverage_ref[line * tiles + tile, j]]
            offset = ring_place(lax.div(slot, per_chip), chips) - home
            offset = jnp.where(offset < 0, offset + chips, offset)
            out.append(jnp.where(lax.rem(slot, per_chip) == core, 0, chips) + offset)
        return out

    chosen = {(level, tile): picks(level, tile) for level in (0, -1, 1) for tile in range(tiles)}

    moves[0].wait()
    zero = jnp.zeros((chans, chans), BF16)

    @pl.loop(0, layers)
    def _(layer):
        for tap in range(3):
            west, centre, east = (kernels[layer, tap, shift].astype(F32) for shift in range(3))
            outer = west + east
            terms = (0.5 * west, 0.25 * (outer + centre), 0.25 * (outer - centre), 0.5 * east)
            for term, value in enumerate(terms):
                value = value.astype(BF16)
                for to in range(2):
                    row = tap + to
                    weight[layer, term, row * chans : (row + 1) * chans, to * chans : (to + 1) * chans] = value
        for term in range(4):
            weight[layer, term, 3 * chans :, :chans] = zero
            weight[layer, term, :chans, chans:] = zero

    for move in moves[1:3] + block_moves:
        move.wait()
    gain = gain_v[...]

    def score(slot, row, size, level, tile):
        amount = size * wide
        part = cells[pl.ds(row, size), tile * wide : (tile + 1) * wide, :].reshape(amount, chans)
        top = None
        for j, which in enumerate(chosen[level, tile]):
            found = jnp.dot(part, keys[which], preferred_element_type=F32)
            scores[slot, :amount, j * kv_rows : (j + 1) * kv_rows] = found
            for lane in range(0, kv_rows, 128):
                piece = found[:, lane : lane + 128]
                top = piece if top is None else jnp.maximum(top, piece)
        tops[slot, :amount] = jnp.broadcast_to(jnp.max(top, -1, keepdims=True), (amount, 128))

    def mix(slot, row, size, level, tile):
        amount = size * wide
        top = tops[slot, :amount]
        probs = [
            jnp.exp2(scores[slot, :amount, lane : lane + 128] - top).astype(BF16)
            for lane in range(0, cover * kv_rows, 128)
        ]
        covered = jnp.concatenate([values[which] for which in chosen[level, tile]], 0)
        summed = jnp.dot(jnp.concatenate(probs, -1), covered, preferred_element_type=F32)
        attended, mass = summed[:, :chans], summed[:, chans:]
        meansq = jnp.mean(attended * attended, -1, keepdims=True)
        part = cells[pl.ds(row, size), tile * wide : (tile + 1) * wide, :].reshape(amount, chans)
        total = part.astype(F32) + gain * attended * lax.rsqrt(meansq + 1e-6 * mass * mass)
        mixed[pl.ds(row, size), tile * wide : (tile + 1) * wide, :] = total.reshape(size, wide, chans)

    score(0, halo, step, 0, 0)

    @pl.loop(0, own // step - 1)
    def _(i):
        row = halo + i * step
        for tile in range(tiles):
            ahead = (tile + 1) % tiles
            score(ahead % 2, row + (step if ahead == 0 else 0), step, 0, ahead)
            mix(tile % 2, row, step, 0, tile)

    for move in moves[3:]:
        move.wait()
    pieces = [(halo + own - step, step, 0, tile) for tile in range(tiles)]
    pieces += [(0, halo, -1, tile) for tile in range(tiles)]
    pieces += [(halo + own, halo, 1, tile) for tile in range(tiles)]
    for at, piece in enumerate(pieces):
        if at + 1 < len(pieces):
            score((at + 1) % 2, *pieces[at + 1])
        mix(at % 2, *piece)

    @pl.when(first)
    def _():
        mixed[:halo] = jnp.zeros((halo, cols, chans), F32)

    @pl.when(last)
    def _():
        mixed[halo + own :] = jnp.zeros((halo, cols, chans), F32)

    def put(dst, pair, amount, even, odd):
        column = lax.rem(lax.broadcasted_iota(jnp.int32, (amount * half, 1), 0), half)
        before = jnp.where(column == 0, 0.0, pltpu.roll(odd, 1, 0))
        after = jnp.where(column == half - 1, 0.0, pltpu.roll(even, amount * half - 1, 0))
        for term, value in enumerate((before - odd, even + odd, odd - even, even - after)):
            dst[term, pl.ds(pair, amount)] = value.astype(BF16).reshape(amount, half, 2 * chans)

    pairs = (own + 2 * halo) // 2

    batch = 4 if pairs % 4 == 0 else 1

    @pl.loop(0, pairs // batch)
    def _(i):
        for pair in range(batch):
            even, odd = (
                jnp.concatenate(
                    [mixed.at[2 * (i * batch + pair) + k][pl.ds(side, half, stride=2), :] for k in range(2)], -1
                )
                for side in range(2)
            )
            put(state_a, i * batch + pair, 1, even, odd)

    source, target = state_a, state_b
    for layer in range(layers):
        pairs -= 1
        group = min(range(GROUP // 2, GROUP + 1), key=lambda size: (-(-pairs // size) * size, -size))
        final = layer == layers - 1
        bias = 0.5 * jnp.concatenate([bias_v[layer : layer + 1, :]] * 2, -1)

        def convolve(at, amount, spare):
            terms = []
            for term in range(4):
                taps = [source[term, pl.ds(at + lower, amount)].reshape(amount * half, 2 * chans) for lower in range(2)]
                terms.append(jnp.dot(jnp.concatenate(taps, -1), weight[layer, term], preferred_element_type=F32))
            centre = terms[1] + bias
            even = centre + terms[2] + terms[0]
            odd = centre - terms[2] - terms[3]
            even = even + even * jnp.tanh(even)
            odd = odd + odd * jnp.tanh(odd)
            if not final:
                put(target, at, amount, even, odd)
                return
            for k in range(amount):
                for side in range(2):
                    one = rows_f32.at[spare + 2 * k + side]
                    one[pl.ds(0, half, stride=2), :] = even[k * half : (k + 1) * half, side * chans : (side + 1) * chans]
                    one[pl.ds(1, half, stride=2), :] = odd[k * half : (k + 1) * half, side * chans : (side + 1) * chans]
            out[pl.ds(2 * at, 2 * amount)] = rows_f32[spare : spare + 2 * amount].astype(BF16)

        @pl.loop(0, pl.cdiv(pairs, group))
        def _(i):
            start = jnp.minimum(i * group, pairs - group)
            subs = -(-group // SUB)
            for sub in range(subs):
                low, high = sub * group // subs, (sub + 1) * group // subs
                convolve(start + low, high - low, 2 * low)
            if final and pairs % group == 0:
                part = pl.ds(2 * start, 2 * group)
                pltpu.make_async_copy(out.at[part], out_hbm.at[part], sem_out.at[i]).start()

        margin = layers - 1 - layer
        if margin:
            blank = jnp.zeros((4, half, chans), BF16)

            @pl.when(first)
            def _():
                for row in range(margin):
                    target[:, row // 2, :, (row % 2) * chans : (row % 2 + 1) * chans] = blank

            @pl.when(last)
            def _():
                for row in range(2 * pairs - margin, 2 * pairs):
                    target[:, row // 2, :, (row % 2) * chans : (row % 2 + 1) * chans] = blank

        source, target = target, source
    if pairs % group == 0:
        for i in range(pairs // group):
            part = slice(2 * i * group, 2 * (i + 1) * group)
            pltpu.make_async_copy(out.at[part], out_hbm.at[part], sem_out.at[i]).wait()
    else:
        move = pltpu.make_async_copy(out, out_hbm, sem_out.at[0])
        move.start()
        move.wait()


def attend_and_convolve(coverage, owner_slot, fine, inner, outer, gain, kernels, bias, blocks):
    own, cols, chans = fine.shape
    halo, count, cover = inner.shape[0], len(blocks), coverage.shape[1]
    tiles = coverage.shape[0] // count
    kv_rows = blocks[0].shape[1]
    amount = STEP * cols // tiles
    total = own + 2 * halo
    state = pltpu.VMEM((4, total // 2, cols // 2, 2 * chans), BF16)
    return pl.pallas_call(
        functools.partial(main_kernel, count, STEP),
        out_shape=jax.ShapeDtypeStruct(fine.shape, BF16),
        in_specs=[SMEM] * 2 + [HBM] * (6 + count),
        out_specs=HBM,
        scratch_shapes=[
            pltpu.VMEM((total, cols, chans), BF16),
            pltpu.VMEM((total, cols, chans), F32),
            pltpu.VMEM((count, chans, kv_rows), BF16),
            pltpu.VMEM((count, kv_rows, 2 * chans), BF16),
            pltpu.VMEM((2, amount, cover * kv_rows), F32),
            pltpu.VMEM((2, amount, 128), F32),
            pltpu.VMEM(gain.shape, F32),
            pltpu.VMEM(kernels.shape, BF16),
            pltpu.VMEM((kernels.shape[0], 4, 4 * chans, 2 * chans), BF16),
            pltpu.VMEM(bias.shape, F32),
            state,
            state,
            pltpu.VMEM((2 * GROUP, cols, chans), F32),
            pltpu.VMEM(fine.shape, BF16),
            pltpu.SemaphoreType.DMA((count, 1 + kv_rows // chans)),
            pltpu.SemaphoreType.DMA((6,)),
            pltpu.SemaphoreType.DMA((own // 2,)),
        ],
        compiler_params=pltpu.CompilerParams(vmem_limit_bytes=LARGE),
        name="attend_and_convolve",
    )(coverage, owner_slot, fine, inner, outer, gain, kernels, bias, *blocks)


def on_device(
    fine, parent, coverage, owner_slot, w_query, w_key, w_value, norm_gain, conv_weight, conv_bias
):
    count = lax.axis_size("row")
    block, inner, outer = encode(parent[0], w_key, w_value, w_query, fine, conv_weight.shape[0])
    swap = lambda array, low: lax.ppermute(
        array, "row", [pair for i in range(low, count - 1, 2) for pair in ((i, i + 1), (i + 1, i))]
    )
    inner = swap(inner, 0)
    outer = swap(outer, 1)
    blocks = gather_blocks(block, count)
    return attend_and_convolve(
        coverage, owner_slot, fine, inner, outer, norm_gain[None], conv_weight, conv_bias, blocks
    )


def solution(mesh):
    placed = (
        P(("groups", "row"), None, None),
        P(("groups", "row"), None, None),
        P("groups", None),
        P("groups"),
        P(),
        P(),
        P(),
        P(),
        P(),
        P(),
    )
    return jax.shard_map(
        on_device,
        mesh=mesh,
        in_specs=placed,
        out_specs=P(("groups", "row"), None, None),
        check_vma=False,
    )
```

```python
import functools
import math

import jax
import jax.numpy as jnp
from jax import lax
from jax.experimental import pallas as pl
from jax.experimental.pallas import tpu as pltpu
from jax.sharding import PartitionSpec as P


BF16, F32 = jnp.bfloat16, jnp.float32
VMEM = pl.BlockSpec(memory_space=pltpu.VMEM)
SMEM = pl.BlockSpec(memory_space=pltpu.SMEM)
ANY = pl.BlockSpec(memory_space=pl.ANY)
HBM = pl.BlockSpec(memory_space=pltpu.HBM)
LARGE = 60 * 2**20
STEP = 16
GROUP = 18
SUB = 4


def encode_kernel(halo, parent_hbm, wk_hbm, wv_hbm, wq_hbm, fine_hbm, out_ref, inner_ref, outer_ref, *rest):
    parent_ref, wk_ref, wv_ref, wq_ref, sem = rest
    own = fine_hbm.shape[0]
    even = lax.rem(lax.axis_index("row"), 2) == 0
    plain = (
        (parent_hbm, parent_ref),
        (wk_hbm, wk_ref),
        (wv_hbm, wv_ref),
        (wq_hbm, wq_ref),
        (fine_hbm.at[pl.ds(jnp.where(even, own - halo, 0), halo)], inner_ref),
        (fine_hbm.at[pl.ds(jnp.where(even, 0, own - halo), halo)], outer_ref),
    )
    moves = [pltpu.make_async_copy(src, dst, sem.at[i]) for i, (src, dst) in enumerate(plain)]
    for move in moves:
        move.start()
    for move in moves[:4]:
        move.wait()
    rows, chans = parent_ref.shape[0], wk_ref.shape[1]
    parent = parent_ref[...]
    keys = jnp.dot(parent, wk_ref[...], preferred_element_type=F32)
    scale = math.log2(math.e) / math.sqrt(chans)
    folded = jnp.dot(wq_ref[...], keys.T.astype(BF16), preferred_element_type=F32) * scale
    values = jnp.dot(parent, wv_ref[...], preferred_element_type=F32).astype(BF16)
    out_ref[:chans, :] = folded.astype(BF16)
    for half in range(rows // chans):
        out_ref[chans:, half * chans : (half + 1) * chans] = values[half * chans : (half + 1) * chans]
    for move in moves[4:]:
        move.wait()


def encode(parent, w_key, w_value, w_query, fine, halo):
    rows, chans = parent.shape[0], w_key.shape[1]
    edge = jax.ShapeDtypeStruct((halo,) + fine.shape[1:], BF16)
    return pl.pallas_call(
        functools.partial(encode_kernel, halo),
        out_shape=[jax.ShapeDtypeStruct((2 * chans, rows), BF16), edge, edge],
        in_specs=[HBM] * 5,
        out_specs=[VMEM] * 3,
        scratch_shapes=[pltpu.VMEM(a.shape, a.dtype) for a in (parent, w_key, w_value, w_query)]
        + [pltpu.SemaphoreType.DMA((6,))],
        compiler_params=pltpu.CompilerParams(vmem_limit_bytes=LARGE),
        name="encode",
    )(parent, w_key, w_value, w_query, fine)


def ring_shape(count):
    per_chip = 2 if count % 2 == 0 else 1
    return per_chip, count // per_chip


def ring_place(chip, chips):
    half = lax.div(chip, 2)
    return jnp.where(lax.rem(chip, 2) == 0, half, chips - 1 - half)


def gather_blocks(block, count):
    per_chip, chips = ring_shape(count)
    order = list(range(0, chips, 2)) + list(range(1, chips, 2))[::-1]

    def step(array, shift):
        pairs = [
            (order[at] * per_chip + core, order[(at + shift) % chips] * per_chip + core)
            for at in range(chips)
            for core in range(per_chip)
        ]
        return lax.ppermute(array, "row", pairs)

    held = {0: block}
    ahead = behind = block
    up, down = chips // 2, (chips - 1) // 2
    for hop in range(1, up + 1):
        ahead = step(ahead, 1)
        held[chips - hop] = ahead
        if hop <= down:
            behind = step(behind, -1)
            held[hop] = behind
    own = [held[offset] for offset in range(chips)]
    if per_chip == 1:
        return own
    partner = [(i, i ^ 1) for i in range(count)]
    others = []
    for array in own:
        others.append(lax.ppermute(array, "row", partner))
    return own + others


def main_kernel(
    count, step, coverage_ref, owner_ref, fine_hbm, inner_hbm, outer_hbm, gain_hbm, kernel_hbm, bias_hbm, *rest
):
    blocks, out_hbm, rest = rest[:count], rest[count], rest[count + 1 :]
    cells, mixed, keys, values, scores, tops, gain_v, kernels, weight, bias_v, state_a, state_b = rest[:12]
    rows_f32, out, sem_kv, sem, sem_out = rest[12:]
    halo, own = inner_hbm.shape[0], fine_hbm.shape[0]
    cols, chans = cells.shape[1:]
    half = cols // 2
    tiles = coverage_ref.shape[1] // count
    cover = coverage_ref.shape[0]
    kv_rows = blocks[0].shape[1]
    layers = weight.shape[0]
    wide = cols // tiles
    per_chip, chips = ring_shape(count)
    position = lax.axis_index("row")
    home = ring_place(lax.div(position, per_chip), chips)
    core = lax.rem(position, per_chip)
    first, last = position == 0, position == count - 1
    even = lax.rem(position, 2) == 0

    plain = [
        (kernel_hbm, kernels),
        (fine_hbm, cells.at[halo : halo + own]),
        (gain_hbm, gain_v),
        (inner_hbm, cells.at[pl.ds(jnp.where(even, halo + own, 0), halo)]),
        (outer_hbm, cells.at[pl.ds(jnp.where(even, 0, halo + own), halo)]),
        (bias_hbm, bias_v),
    ]
    moves = [pltpu.make_async_copy(src, dst, sem.at[i]) for i, (src, dst) in enumerate(plain)]
    for move in moves[:3]:
        move.start()
    block_moves = []
    for at, ref in enumerate(blocks):
        block_moves.append(pltpu.make_async_copy(ref.at[0:chans], keys.at[at], sem_kv.at[at, 0]))
        for part in range(kv_rows // chans):
            block_moves.append(
                pltpu.make_async_copy(
                    ref.at[chans : 2 * chans, part * chans : (part + 1) * chans],
                    values.at[at, part * chans : (part + 1) * chans, 0:chans],
                    sem_kv.at[at, 1 + part],
                )
            )
    for move in block_moves + moves[3:]:
        move.start()
    values[:, :, chans:] = jnp.ones(values.shape[:2] + (values.shape[2] - chans,), BF16)

    def picks(level, tile):
        line = jnp.minimum(jnp.maximum(position + level, 0), count - 1)
        out = []
        for j in range(cover):
            slot = owner_ref[coverage_ref[j, line * tiles + tile]]
            offset = ring_place(lax.div(slot, per_chip), chips) - home
            offset = jnp.where(offset < 0, offset + chips, offset)
            out.append(jnp.where(lax.rem(slot, per_chip) == core, 0, chips) + offset)
        return out

    chosen = {(level, tile): picks(level, tile) for level in (0, -1, 1) for tile in range(tiles)}

    moves[0].wait()
    zero = jnp.zeros((chans, chans), BF16)

    @pl.loop(0, layers)
    def _(layer):
        for tap in range(3):
            west, centre, east = (kernels[layer, tap, shift].astype(F32) for shift in range(3))
            outer = west + east
            terms = (0.5 * west, 0.25 * (outer + centre), 0.25 * (outer - centre), 0.5 * east)
            for term, value in enumerate(terms):
                value = value.astype(BF16)
                for to in range(2):
                    row = tap + to
                    weight[layer, term, row * chans : (row + 1) * chans, to * chans : (to + 1) * chans] = value
        for term in range(4):
            weight[layer, term, 3 * chans :, :chans] = zero
            weight[layer, term, :chans, chans:] = zero

    for move in moves[1:3] + block_moves:
        move.wait()
    gain = gain_v[...]

    def score(slot, row, size, level, tile):
        amount = size * wide
        part = cells[pl.ds(row, size), tile * wide : (tile + 1) * wide, :].reshape(amount, chans)
        top = None
        for j, which in enumerate(chosen[level, tile]):
            found = jnp.dot(part, keys[which], preferred_element_type=F32)
            scores[slot, :amount, j * kv_rows : (j + 1) * kv_rows] = found
            for lane in range(0, kv_rows, 128):
                piece = found[:, lane : lane + 128]
                top = piece if top is None else jnp.maximum(top, piece)
        tops[slot, :amount] = jnp.broadcast_to(jnp.max(top, -1, keepdims=True), (amount, 128))

    def mix(slot, row, size, level, tile):
        amount = size * wide
        top = tops[slot, :amount]
        probs = [
            jnp.exp2(scores[slot, :amount, lane : lane + 128] - top).astype(BF16)
            for lane in range(0, cover * kv_rows, 128)
        ]
        covered = jnp.concatenate([values[which] for which in chosen[level, tile]], 0)
        summed = jnp.dot(jnp.concatenate(probs, -1), covered, preferred_element_type=F32)
        attended, mass = summed[:, :chans], summed[:, chans:]
        meansq = jnp.mean(attended * attended, -1, keepdims=True)
        part = cells[pl.ds(row, size), tile * wide : (tile + 1) * wide, :].reshape(amount, chans)
        total = part.astype(F32) + gain * attended * lax.rsqrt(meansq + 1e-6 * mass * mass)
        mixed[pl.ds(row, size), tile * wide : (tile + 1) * wide, :] = total.reshape(size, wide, chans)

    score(0, halo, step, 0, 0)

    @pl.loop(0, own // step - 1)
    def _(i):
        row = halo + i * step
        for tile in range(tiles):
            ahead = (tile + 1) % tiles
            score(ahead % 2, row + (step if ahead == 0 else 0), step, 0, ahead)
            mix(tile % 2, row, step, 0, tile)

    for move in moves[3:]:
        move.wait()
    pieces = [(halo + own - step, step, 0, tile) for tile in range(tiles)]
    pieces += [(0, halo, -1, tile) for tile in range(tiles)]
    pieces += [(halo + own, halo, 1, tile) for tile in range(tiles)]
    for at, piece in enumerate(pieces):
        if at + 1 < len(pieces):
            score((at + 1) % 2, *pieces[at + 1])
        mix(at % 2, *piece)

    @pl.when(first)
    def _():
        mixed[:halo] = jnp.zeros((halo, cols, chans), F32)

    @pl.when(last)
    def _():
        mixed[halo + own :] = jnp.zeros((halo, cols, chans), F32)

    def put(dst, pair, amount, even, odd):
        column = lax.rem(lax.broadcasted_iota(jnp.int32, (amount * half, 1), 0), half)
        before = jnp.where(column == 0, 0.0, pltpu.roll(odd, 1, 0))
        after = jnp.where(column == half - 1, 0.0, pltpu.roll(even, amount * half - 1, 0))
        for term, value in enumerate((before - odd, even + odd, odd - even, even - after)):
            dst[term, pl.ds(pair, amount)] = value.astype(BF16).reshape(amount, half, 2 * chans)

    pairs = (own + 2 * halo) // 2

    batch = 4 if pairs % 4 == 0 else 1

    @pl.loop(0, pairs // batch)
    def _(i):
        for pair in range(batch):
            even, odd = (
                jnp.concatenate(
                    [mixed.at[2 * (i * batch + pair) + k][pl.ds(side, half, stride=2), :] for k in range(2)], -1
                )
                for side in range(2)
            )
            put(state_a, i * batch + pair, 1, even, odd)

    source, target = state_a, state_b
    for layer in range(layers):
        pairs -= 1
        group = min(range(GROUP // 2, GROUP + 1), key=lambda size: (-(-pairs // size) * size, -size))
        final = layer == layers - 1
        bias = 0.5 * jnp.concatenate([bias_v[layer : layer + 1, :]] * 2, -1)

        def convolve(at, amount, spare):
            terms = []
            for term in range(4):
                taps = [source[term, pl.ds(at + lower, amount)].reshape(amount * half, 2 * chans) for lower in range(2)]
                terms.append(jnp.dot(jnp.concatenate(taps, -1), weight[layer, term], preferred_element_type=F32))
            centre = terms[1] + bias
            even = centre + terms[2] + terms[0]
            odd = centre - terms[2] - terms[3]
            even = even + even * jnp.tanh(even)
            odd = odd + odd * jnp.tanh(odd)
            if not final:
                put(target, at, amount, even, odd)
                return
            for k in range(amount):
                for side in range(2):
                    one = rows_f32.at[spare + 2 * k + side]
                    one[pl.ds(0, half, stride=2), :] = even[k * half : (k + 1) * half, side * chans : (side + 1) * chans]
                    one[pl.ds(1, half, stride=2), :] = odd[k * half : (k + 1) * half, side * chans : (side + 1) * chans]
            out[pl.ds(2 * at, 2 * amount)] = rows_f32[spare : spare + 2 * amount].astype(BF16)

        @pl.loop(0, pl.cdiv(pairs, group))
        def _(i):
            start = jnp.minimum(i * group, pairs - group)
            subs = -(-group // SUB)
            for sub in range(subs):
                low, high = sub * group // subs, (sub + 1) * group // subs
                convolve(start + low, high - low, 2 * low)
            if final and pairs % group == 0:
                part = pl.ds(2 * start, 2 * group)
                pltpu.make_async_copy(out.at[part], out_hbm.at[part], sem_out.at[i]).start()

        margin = layers - 1 - layer
        if margin:
            blank = jnp.zeros((4, half, chans), BF16)

            @pl.when(first)
            def _():
                for row in range(margin):
                    target[:, row // 2, :, (row % 2) * chans : (row % 2 + 1) * chans] = blank

            @pl.when(last)
            def _():
                for row in range(2 * pairs - margin, 2 * pairs):
                    target[:, row // 2, :, (row % 2) * chans : (row % 2 + 1) * chans] = blank

        source, target = target, source
    if pairs % group == 0:
        for i in range(pairs // group):
            part = slice(2 * i * group, 2 * (i + 1) * group)
            pltpu.make_async_copy(out.at[part], out_hbm.at[part], sem_out.at[i]).wait()
    else:
        move = pltpu.make_async_copy(out, out_hbm, sem_out.at[0])
        move.start()
        move.wait()


def attend_and_convolve(coverage, owner_slot, fine, inner, outer, gain, kernels, bias, blocks):
    own, cols, chans = fine.shape
    halo, count, cover = inner.shape[0], len(blocks), coverage.shape[0]
    tiles = coverage.shape[1] // count
    kv_rows = blocks[0].shape[1]
    amount = STEP * cols // tiles
    total = own + 2 * halo
    state = pltpu.VMEM((4, total // 2, cols // 2, 2 * chans), BF16)
    return pl.pallas_call(
        functools.partial(main_kernel, count, STEP),
        out_shape=jax.ShapeDtypeStruct(fine.shape, BF16),
        in_specs=[SMEM] * 2 + [HBM] * (6 + count),
        out_specs=HBM,
        scratch_shapes=[
            pltpu.VMEM((total, cols, chans), BF16),
            pltpu.VMEM((total, cols, chans), F32),
            pltpu.VMEM((count, chans, kv_rows), BF16),
            pltpu.VMEM((count, kv_rows, 2 * chans), BF16),
            pltpu.VMEM((2, amount, cover * kv_rows), F32),
            pltpu.VMEM((2, amount, 128), F32),
            pltpu.VMEM(gain.shape, F32),
            pltpu.VMEM(kernels.shape, BF16),
            pltpu.VMEM((kernels.shape[0], 4, 4 * chans, 2 * chans), BF16),
            pltpu.VMEM(bias.shape, F32),
            state,
            state,
            pltpu.VMEM((2 * GROUP, cols, chans), F32),
            pltpu.VMEM(fine.shape, BF16),
            pltpu.SemaphoreType.DMA((count, 1 + kv_rows // chans)),
            pltpu.SemaphoreType.DMA((6,)),
            pltpu.SemaphoreType.DMA((own // 2,)),
        ],
        compiler_params=pltpu.CompilerParams(vmem_limit_bytes=LARGE),
        name="attend_and_convolve",
    )(coverage, owner_slot, fine, inner, outer, gain, kernels, bias, *blocks)


def on_device(
    fine, parent, coverage, owner_slot, w_query, w_key, w_value, norm_gain, conv_weight, conv_bias
):
    count = lax.axis_size("row")
    block, inner, outer = encode(parent[0], w_key, w_value, w_query, fine, conv_weight.shape[0])
    swap = lambda array, low: lax.ppermute(
        array, "row", [pair for i in range(low, count - 1, 2) for pair in ((i, i + 1), (i + 1, i))]
    )
    inner = swap(inner, 0)
    outer = swap(outer, 1)
    blocks = gather_blocks(block, count)
    return attend_and_convolve(
        coverage.T, owner_slot, fine, inner, outer, norm_gain[None], conv_weight, conv_bias, blocks
    )


def solution(mesh):
    placed = (
        P(("groups", "row"), None, None),
        P(("groups", "row"), None, None),
        P("groups", None),
        P("groups"),
        P(),
        P(),
        P(),
        P(),
        P(),
        P(),
    )
    return jax.shard_map(
        on_device,
        mesh=mesh,
        in_specs=placed,
        out_specs=P(("groups", "row"), None, None),
        check_vma=False,
    )
```
